256 devices in a mesh: dp: 8 (over z_lo, x), seq: 32 (over z_hi, y, core).
Axes of the slice: x: 4, y: 4, z: 8 (z_hi: 4, z_lo: 2; z = z_hi * 2 + z_lo), core: 2. Of those that a mesh axis runs over, the one named last changes fastest.
Arguments:
- tiles: bfloat16 [8, 16, 64, 4, 1024], P('dp', None, 'seq'), may hold values from -6 to 6
- patch_index: int32 [8, 16, 64, 4], P('dp', None, 'seq'), may hold values from 0 to 255
- pos_table: bfloat16 [256, 1024], replicated, may hold values from -6 to 6
- depth_kernel: bfloat16 [2, 27, 1024], replicated, may hold values from -1.25 to 1.25
- enc_gain: bfloat16 [2, 1024], replicated, may hold values from 0.099609375 to 1.8984375
- point_weight: bfloat16 [2, 1024, 1024], replicated, may hold values from -0.1875 to 0.1875
- action_ids: int32 [8, 16], replicated, may hold values from 0 to 7
- w_in: bfloat16 [1024, 5120], P('seq', 'dp'), may hold values from -0.1875 to 0.1875
- action_table: bfloat16 [8, 5120], P(None, 'dp'), may hold values from -6 to 6
- dyn_gain: bfloat16 [5120], P('dp'), may hold values from 0.099609375 to 1.8984375
- w_query: bfloat16 [5120, 5120], P('seq', 'dp'), may hold values from -0.078125 to 0.078125
- w_keyval: bfloat16 [5120, 2, 1024], P('seq', None, 'dp'), may hold values from -0.078125 to 0.078125
- seq_order: int32 [4], replicated, may hold values from 0 to 3, each once
Outputs:
- attended: bfloat16 [8, 16, 64, 4, 5120], P(None, None, 'seq', None, 'dp')
The draws below stay inside these ranges and needn't reach their ends.
Inputs may be any that keep to these rules, and one draw needn't show every extreme that they name: `seq_order`: each of 0 to 3 appears once.
All inputs are finite; a program needn't handle non-finite values.
Results may differ from the reference program's by a relative error of at most 0.012.
Values may be sent and summed in bfloat16 or wider, within the bound.
No kernel may reach another device: no remote copies, remote signals or barrier semaphores. Data moves between devices by JAX's collectives and lax.ppermute only.
A program may use at most 128 MiB of HBM per device.

```python
import jax
import jax.numpy as jnp
from jax import lax

ENC = 1024
DIM = 5120
HEAD = 128
Q_HEADS = 40
KV_HEADS = 8
ACTIONS = 8
FRAMES = 16
LAYERS = 2
COLS = 4
CLIPS = 8
ROWS = 64
POSITIONS = 256


def with_ends(values, key, low, top_value):
    dims = values.shape
    spot = [jax.random.randint(jax.random.fold_in(key, axis), (), 0, dims[axis]) for axis in range(len(dims))]
    values = values.at[tuple(spot)].set(low)
    longest = dims.index(max(dims))
    spot[longest] = (spot[longest] + 1) % dims[longest]
    return values.at[tuple(spot)].set(top_value)


def steps_of(stream_key, shape, split, least, high):
    factor_of, own = 1.0, jax.random.fold_in(stream_key, 6)
    for dim, blocks in split:
        draws = jnp.exp(jax.random.uniform(jax.random.fold_in(own, dim), (blocks,), jnp.float32, least / len(split), high / len(split)))
        factor_of = factor_of * jnp.repeat(draws, shape[dim] // blocks).reshape([-1 if axis == dim else 1 for axis in range(len(shape))])
    return factor_of


def scatter_about(stream_key, dims, width, limit, shards=(), kind=jnp.bfloat16):
    entries = width * jax.random.normal(stream_key, dims, jnp.float32)
    if shards:
        entries = entries * steps_of(stream_key, dims, shards, -0.22, 0.18)
    return jnp.clip(entries, -limit, limit).astype(kind)


def setup_inputs(seed: int = 0) -> dict:
    arg_keys = jax.random.split(jax.random.key(seed), 14)
    return {
        "tiles": scatter_about(arg_keys[0], (CLIPS, FRAMES, ROWS, COLS, ENC), 1.0, 6.0, ((0, 8), (2, 32))),
        "patch_index": with_ends(jax.random.randint(arg_keys[1], (CLIPS, FRAMES, ROWS, COLS), 0, POSITIONS), jax.random.fold_in(arg_keys[1], 1), 0, POSITIONS - 1).astype(jnp.int32),
        "pos_table": scatter_about(arg_keys[2], (POSITIONS, ENC), 1.0, 6.0),
        "depth_kernel": scatter_about(arg_keys[3], (LAYERS, 27, ENC), 27 ** -0.5, 1.25),
        "enc_gain": jnp.clip(1.0 + 0.18 * jax.random.normal(arg_keys[4], (LAYERS, ENC), jnp.float32), 0.099609375, 1.8984375).astype(jnp.bfloat16),
        "point_weight": scatter_about(arg_keys[5], (LAYERS, ENC, ENC), ENC ** -0.5, 0.1875),
        "action_ids": with_ends(jax.random.randint(arg_keys[6], (CLIPS, FRAMES), 0, ACTIONS), jax.random.fold_in(arg_keys[6], 1), 0, ACTIONS - 1).astype(jnp.int32),
        "w_in": scatter_about(arg_keys[7], (ENC, DIM), ENC ** -0.5, 0.1875, ((0, 32), (1, 8))),
        "action_table": scatter_about(arg_keys[8], (ACTIONS, DIM), 1.0, 6.0, ((1, 8),)),
        "dyn_gain": jnp.clip(1.0 + 0.18 * jax.random.normal(arg_keys[9], (DIM,), jnp.float32), 0.099609375, 1.8984375).astype(jnp.bfloat16),
        "w_query": scatter_about(arg_keys[10], (DIM, DIM), DIM ** -0.5, 0.078125, ((0, 32), (1, 8))),
        "w_keyval": scatter_about(arg_keys[11], (DIM, 2, KV_HEADS * HEAD), DIM ** -0.5, 0.078125, ((0, 32), (2, 8))),
        "seq_order": jax.random.permutation(arg_keys[12], COLS).astype(jnp.int32),
    }


def depth_block(padded, kernel, gains, weight):
    frames = padded.shape[1]
    height = padded.shape[2] - 2
    breadth = padded.shape[3]
    channels = padded.shape[4]
    framed = jnp.pad(padded.astype(jnp.float32), ((0, 0), (2, 0), (0, 0), (1, 1), (0, 0)))
    summed = jnp.zeros((padded.shape[0], frames, height, breadth, channels), jnp.float32)
    for time_tap in range(3):
        for row_tap in range(3):
            for col_tap in range(3):
                window = framed[:, time_tap:time_tap + frames, row_tap:row_tap + height, col_tap:col_tap + breadth, :]
                summed = summed + window * kernel[9 * time_tap + 3 * row_tap + col_tap].astype(jnp.float32)
    factor = lax.rsqrt(lax.optimization_barrier(jnp.mean(summed * summed, axis=-1, keepdims=True)) + 1e-05)
    normed = (summed * factor * gains.astype(jnp.float32)).astype(jnp.bfloat16)
    projected = jnp.dot(normed.reshape(-1, channels), weight, preferred_element_type=jnp.float32).reshape(summed.shape)
    centre = padded[:, :, 1:-1].astype(jnp.float32)
    return (centre + jax.nn.gelu(projected)).astype(jnp.bfloat16)

def temporal_mix(query_heads, key_heads, value_heads):
    frames = query_heads.shape[1]
    query_unit = query_heads * lax.rsqrt(lax.optimization_barrier(jnp.mean(query_heads * query_heads, axis=-1, keepdims=True)) + 1e-06)
    key_unit = key_heads * lax.rsqrt(lax.optimization_barrier(jnp.mean(key_heads * key_heads, axis=-1, keepdims=True)) + 1e-06)
    scores = jnp.einsum('cfpkgh,ctpkh->cpkgft', query_unit, key_unit, precision=lax.Precision.HIGHEST) * HEAD ** (-0.5)
    causal = jnp.arange(frames, dtype=jnp.int32)[:, None] >= jnp.arange(frames, dtype=jnp.int32)[None, :]
    raised = jnp.where(causal, jnp.exp(scores), 0.0)
    shares = (raised / lax.optimization_barrier(jnp.sum(raised, axis=-1, keepdims=True))).astype(jnp.bfloat16)
    mixed = jnp.einsum('cpkgft,ctpkh->cfpkgh', shares.astype(jnp.float32), value_heads.astype(jnp.float32), precision=lax.Precision.HIGHEST)
    return mixed.astype(jnp.bfloat16)

def reference(tiles, patch_index, pos_table, depth_kernel, enc_gain, point_weight, action_ids, w_in, action_table, dyn_gain, w_query, w_keyval, seq_order):
    placed = jnp.take(pos_table, patch_index, axis=0).astype(jnp.float32)
    hidden = (tiles.astype(jnp.float32) + placed).astype(jnp.bfloat16)
    for block_idx in range(LAYERS):
        padded = jnp.pad(hidden, ((0, 0), (0, 0), (1, 1), (0, 0), (0, 0)))
        hidden = depth_block(padded, depth_kernel[block_idx], enc_gain[block_idx], point_weight[block_idx])
    group = Q_HEADS // KV_HEADS
    cells = ROWS * COLS

    def one_clip(inputs_pair):
        latent, frame_ids = inputs_pair
        embed = jnp.dot(latent.reshape(-1, ENC), w_in, preferred_element_type=jnp.float32).reshape(FRAMES, cells, DIM)
        embed = embed + jnp.take(action_table, frame_ids, axis=0).astype(jnp.float32)[:, None, :]
        embed = jax.nn.gelu(embed)
        factor = lax.rsqrt(lax.optimization_barrier(jnp.mean(embed * embed, axis=-1, keepdims=True)) + 1e-05)
        normed = (embed * factor * dyn_gain.astype(jnp.float32)).astype(jnp.bfloat16).reshape(-1, DIM)
        query = jnp.dot(normed, w_query, preferred_element_type=jnp.float32)
        keyval = jnp.dot(normed, w_keyval.reshape(DIM, -1), preferred_element_type=jnp.float32)
        query_heads = query.reshape(1, FRAMES, cells, KV_HEADS, group, HEAD)
        pairs = keyval.reshape(1, FRAMES, cells, 2, KV_HEADS, HEAD)
        mixed = temporal_mix(query_heads, pairs[:, :, :, 0], pairs[:, :, :, 1].astype(jnp.bfloat16))
        return mixed.reshape(FRAMES, ROWS, COLS, DIM)
    mixed_all = lax.map(one_clip, (hidden, action_ids))
    return jnp.take(mixed_all, seq_order, axis=3)
```

```python
import functools

import jax
import jax.numpy as jnp
from jax import lax
from jax.experimental import pallas as pl
from jax.experimental.pallas import tpu as pltpu
from jax.sharding import Mesh
from jax.sharding import PartitionSpec as P

DIM = 5120
HEAD = 128
GROUP = 5
FRAMES = 16
COLS = 4
TOKENS = 128
CLIPS = 8
BF = jnp.bfloat16
F32 = jnp.float32
VMEM_LIMIT = 56 * 1024 * 1024
SEQ = ("zh", "y", "c")
DP = ("zl", "x")


def params(**kw):
    return pltpu.CompilerParams(vmem_limit_bytes=VMEM_LIMIT, **kw)


def cost(flops, bytes_accessed, transcendentals=0):
    return pl.CostEstimate(
        flops=int(flops), bytes_accessed=int(bytes_accessed), transcendentals=int(transcendentals)
    )


def gelu(x):
    inner = x * (0.7978845608028654 + 0.035677408136300125 * (x * x))
    half = 0.5 * x
    return half + half * jnp.tanh(inner)


def place_kernel(index_ref, tiles_ref, table_ref, out_ref):
    positions = table_ref.shape[0]
    pick = lax.broadcasted_iota(jnp.int32, (positions, TOKENS), 0) == index_ref[...]
    placed = lax.dot_general(
        pick.astype(BF), table_ref[...], (((0,), (0,)), ((), ())), preferred_element_type=F32
    )
    x0 = (tiles_ref[...].astype(F32) + placed).astype(BF)
    row = lax.broadcasted_iota(jnp.int32, (TOKENS, TOKENS), 0)
    col = lax.broadcasted_iota(jnp.int32, (TOKENS, TOKENS), 1)
    order = (col == (row & 15) * 8 + (row >> 4)).astype(BF)
    out_ref[...] = jnp.dot(order, x0, preferred_element_type=F32).astype(BF)


def place(tiles, index, table):
    return pl.pallas_call(
        place_kernel,
        out_shape=jax.ShapeDtypeStruct(tiles.shape, BF),
        compiler_params=params(),
        cost_estimate=cost(2 * 128 * 384 * 1024, 2**20),
        name="place",
    )(index, tiles, table)


def conv_norm(shifted, conv, kernel, gain, rows):
    channels = conv.shape[-1]
    total = jnp.zeros((rows * COLS, FRAMES, 128), F32)

    def step(block, total):
        lanes = pl.ds(pl.multiple_of(block * 128, 128), 128)
        taps = kernel[:, lanes].astype(F32)
        squares = []
        for r in range(rows):
            for w in range(COLS):
                acc = jnp.zeros((FRAMES, 128), F32)
                for k in range(3):
                    if not 0 <= w + k - 1 < COLS:
                        continue
                    for b in range(3):
                        for a in range(3):
                            tap = 9 * a + 3 * b + k
                            acc = acc + shifted[a, r + b, w + k - 1, :, lanes] * taps[tap : tap + 1]
                conv[r * COLS + w, :, lanes] = acc
                squares.append(acc * acc)
        return total + jnp.stack(squares)

    total = lax.fori_loop(0, channels // 128, step, total)
    mean = jnp.sum(total, axis=-1, keepdims=True) / channels
    factor = lax.rsqrt(mean + 1e-05)
    return (conv[: rows * COLS] * factor * gain.astype(F32)).astype(BF)


def shift_into(shifted, row, value):
    frame = lax.broadcasted_iota(jnp.int32, value.shape, 1)
    shifted[2, row] = value
    shifted[1, row] = jnp.where(frame >= 1, pltpu.roll(value, 1, 1), 0.0)
    shifted[0, row] = jnp.where(frame >= 2, pltpu.roll(value, 2, 1), 0.0)


def encoder_kernel(edge_ref, low_ref, own_ref, high_ref, depth_ref, gain_ref, weight_ref, out_ref, shifted, conv):
    row_tokens = COLS * FRAMES
    channels = own_ref.shape[-1]
    sources = [(ref, half) for ref in (low_ref, own_ref, high_ref) for half in range(2)]

    def rows_of(ref, half):
        return ref[half * row_tokens : (half + 1) * row_tokens].astype(F32)

    for row, (ref, half) in enumerate(sources):
        shift_into(shifted, row, rows_of(ref, half).reshape(COLS, FRAMES, channels))
    normed = conv_norm(shifted, conv, depth_ref.at[0], gain_ref[0:1], 4)
    projected = jnp.dot(normed.reshape(4 * row_tokens, channels), weight_ref[0], preferred_element_type=F32)
    hidden = []
    for i, (ref, half) in enumerate(sources[1:5]):
        x = rows_of(ref, half) + gelu(projected[i * row_tokens : (i + 1) * row_tokens])
        x = x.astype(BF).astype(F32)
        if i == 0:
            x = jnp.where(edge_ref[0] == 0, 0.0, x)
        if i == 3:
            x = jnp.where(edge_ref[1] == 0, 0.0, x)
        hidden.append(x)
    for row, x in enumerate(hidden):
        shift_into(shifted, row, x.reshape(COLS, FRAMES, channels))
    normed = conv_norm(shifted, conv, depth_ref.at[1], gain_ref[1:2], 2)
    projected = jnp.dot(normed.reshape(2 * row_tokens, channels), weight_ref[1], preferred_element_type=F32)
    centre = shifted[2, 1:3].reshape(2 * row_tokens, channels)
    out_ref[...] = (centre + gelu(projected)).astype(BF)


def encoder(edges, low, own, high, depth_kernel, gains, weights):
    channels = own.shape[-1]
    vmem = pl.BlockSpec(memory_space=pltpu.VMEM)
    return pl.pallas_call(
        encoder_kernel,
        out_shape=jax.ShapeDtypeStruct(own.shape, BF),
        in_specs=[pl.BlockSpec(memory_space=pltpu.SMEM)] + [vmem] * 6,
        out_specs=vmem,
        scratch_shapes=[
            pltpu.VMEM((3, 6, COLS, FRAMES, channels), F32),
            pltpu.VMEM((4 * COLS, FRAMES, channels), F32),
        ],
        compiler_params=params(),
        cost_estimate=cost(2 * 384 * 1024 * 1024 * 4, 6 * 2**20),
        name="encoder",
    )(edges, low, own, high, depth_kernel, gains, weights)


def embed_kernel(latent_ref, pick_ref, first_ref, second_ref, out_ref, squares_ref):
    channels = latent_ref.shape[1]
    width = first_ref.shape[1]
    tile = 256
    tokens = latent_ref.shape[0]

    def columns(lo, hi, start, size):
        parts = []
        for i, ref in enumerate((first_ref, second_ref)):
            left, right = max(start, i * width), min(start + size, (i + 1) * width)
            if left < right:
                parts.append(ref[lo:hi, left - i * width : right - i * width])
        return parts[0] if len(parts) == 1 else jnp.concatenate(parts, axis=1)

    total = jnp.zeros((tokens, 128), F32)
    for start in range(0, 2 * width, tile):
        side = columns(channels, channels + 16, start, tile)
        action = jnp.dot(pick_ref[...], side, preferred_element_type=F32)
        gain = side[8:9].astype(F32)
        product = jnp.dot(latent_ref[...], columns(0, channels, start, tile), preferred_element_type=F32)
        cells = tokens // TOKENS
        product = product.reshape(cells, TOKENS // FRAMES, FRAMES, tile) + action.reshape(cells, 1, FRAMES, tile)
        value = gelu(product.reshape(tokens, tile))
        squares = value * value
        total = total + (squares[:, :128] + squares[:, 128:])
        out_ref[:, start : start + tile] = (value * gain).astype(BF)
    squares_ref[...] = total


def embed(latents, pick, first, second):
    tokens, channels = latents.shape
    width = first.shape[1]
    return pl.pallas_call(
        embed_kernel,
        out_shape=(
            jax.ShapeDtypeStruct((tokens, 2 * width), BF),
            jax.ShapeDtypeStruct((tokens, 128), F32),
        ),
        compiler_params=params(),
        cost_estimate=cost(2 * tokens * channels * 2 * width, 8 * 2**20),
        name="embed",
    )(latents, pick, first, second)


def mix_kernel(place_ref, order_ref, *refs):
    inputs, weight_ref, squares = refs[:4], refs[4], refs[5:9]
    out_ref, acc = refs[9], refs[10]
    j = pl.program_id(0)
    for k in range(4):
        @pl.when(j // 2 == k)
        def _(k=k):
            part = jnp.dot(inputs[k][...], weight_ref[...], preferred_element_type=F32)

            if k == 0:
                @pl.when(j == 0)
                def _():
                    acc[...] = part

                @pl.when(j != 0)
                def _():
                    acc[...] += part
            else:
                acc[...] += part

    @pl.when(j == pl.num_programs(0) - 1)
    def _():
        row = lax.broadcasted_iota(jnp.int32, (TOKENS, TOKENS), 0)
        col = lax.broadcasted_iota(jnp.int32, (TOKENS, TOKENS), 1)
        causal = ((row >> 4) == (col >> 4)) & ((col & 15) <= (row & 15))
        slot = row & 3
        source = jnp.where(
            slot < 2,
            jnp.where(slot == 0, order_ref[0], order_ref[1]),
            jnp.where(slot == 2, order_ref[2], order_ref[3]),
        )
        order = (col == (((row >> 2) & 1) * 4 + source) * 16 + (row >> 3)).astype(BF)
        ones = jnp.ones((HEAD, HEAD), BF)

        def mean_square(x):
            return jnp.dot((x * x).astype(BF), ones, preferred_element_type=F32) * (1.0 / HEAD)

        def clip(c, _):
            rows = pl.ds(pl.multiple_of(c * TOKENS, TOKENS), TOKENS)
            total = sum(s[rows] for s in squares)
            factor = lax.rsqrt(jnp.sum(total, axis=-1, keepdims=True) / DIM + 1e-05)
            queries = []
            for h in range(GROUP):
                q = acc[rows, h * HEAD : (h + 1) * HEAD] * factor
                queries.append((q * lax.rsqrt(mean_square(q) + 1e-06)).astype(BF))
            key = acc[rows, GROUP * HEAD : (GROUP + 1) * HEAD] * factor
            key = (key * lax.rsqrt(mean_square(key) + 1e-06) * HEAD ** (-0.5)).astype(BF)
            value = (acc[rows, (GROUP + 1) * HEAD : (GROUP + 2) * HEAD] * factor).astype(BF)
            value = jnp.concatenate([value, ones], axis=1)
            for h in range(GROUP):
                score = lax.dot_general(
                    queries[h], key, (((1,), (1,)), ((), ())), preferred_element_type=F32
                )
                raised = jnp.where(causal, jnp.exp(score), 0.0).astype(BF)
                both = jnp.dot(raised, value, preferred_element_type=F32)
                mixed = (both[:, :HEAD] / both[:, HEAD:]).astype(BF)
                placed = jnp.dot(order, mixed, preferred_element_type=F32).astype(BF)
                out_ref[rows, h * HEAD : (h + 1) * HEAD] = placed
            return 0

        lax.fori_loop(0, CLIPS, clip, 0)


def mix(where, order, inputs, weight, squares):
    tokens = inputs[0].shape[0]
    width = inputs[0].shape[1] // 2
    out_width = GROUP * HEAD
    whole = weight.shape[1]

    def input_map(k):
        return lambda j, where, order: (0, jnp.clip(j - 2 * k, 0, 1))

    def weight_map(j, where, order):
        side = jnp.where(j % 2 == 0, where[1], 1 - where[1])
        return side * 4 + (where[0] + j // 2) % 4, 0

    def fixed(j, where, order):
        return 0, 0

    return pl.pallas_call(
        mix_kernel,
        out_shape=jax.ShapeDtypeStruct((tokens, out_width), BF),
        grid_spec=pltpu.PrefetchScalarGridSpec(
            num_scalar_prefetch=2,
            grid=(8,),
            in_specs=[pl.BlockSpec((tokens, width), input_map(k)) for k in range(4)]
            + [pl.BlockSpec((width, whole), weight_map)]
            + [pl.BlockSpec((tokens, 128), fixed)] * 4,
            out_specs=pl.BlockSpec((tokens, out_width), fixed),
            scratch_shapes=[pltpu.VMEM((tokens, whole), F32)],
        ),
        compiler_params=params(dimension_semantics=("arbitrary",)),
        cost_estimate=cost(2 * tokens * DIM * whole, 24 * 2**20),
        name="mix",
    )(where, order, *inputs, weight, *squares)


def shift(a, axis, by):
    n = lax.axis_size(axis)
    return lax.ppermute(a, axis, [(i, (i + by) % n) for i in range(n)])


def from_(a, axis, k):
    return shift(a, axis, -k)


def natural(blocks, axis, dim=0):
    n = len(blocks)
    stacked = jnp.stack(blocks + blocks[:-1], axis=dim)
    return lax.dynamic_slice_in_dim(stacked, (n - lax.axis_index(axis)) % n, n, dim)


def ring4(a, axis):
    plus, minus = from_(a, axis, 1), from_(a, axis, -1)
    half = a.shape[0] // 2
    far = jnp.concatenate([from_(minus[:half], axis, -1), from_(plus[half:], axis, 1)], 0)
    return [a, plus, far, minus]


def w_in_pieces(w, side):
    c, zl = lax.axis_index("c"), lax.axis_index("zl")
    other = shift(w, "c", 1)
    pair = jnp.where(c == 0, jnp.concatenate([w, other], 0), jnp.concatenate([other, w], 0))
    pair = jnp.concatenate([pair, side], 0)
    sent = lax.ppermute(pair, ("zl", "c"), [(0, 2), (3, 1)])
    block = jnp.where(zl == c, pair, sent)
    rows = 2 * w.shape[0]
    block, side = block[:rows], block[rows:]
    z = natural([block] + [from_(block, "zh", k) for k in (1, 2, 3)], "zh")
    y = natural(ring4(z, "y"), "y", 1)
    full = jnp.concatenate([y.reshape(-1, w.shape[1]), side], 0)
    mine = ring4(full, "x")
    return mine, [shift(p, "c", 1) for p in mine]


def body(
    tiles, patch_index, pos_table, depth_kernel, enc_gain, point_weight, action_ids,
    w_in, action_table, dyn_gain, w_query, w_keyval, seq_order,
):
    channels = tiles.shape[-1]
    seq = lax.axis_index(SEQ)
    seqs = lax.axis_size(SEQ)
    weight = jnp.concatenate([w_query, w_keyval.reshape(w_keyval.shape[0], -1)], axis=1)
    weight = lax.all_gather(weight, SEQ, axis=0, tiled=True)

    side = jnp.concatenate(
        [action_table, dyn_gain[None], jnp.zeros((7, dyn_gain.shape[0]), BF)], axis=0
    )
    mine, others = w_in_pieces(w_in, side)

    x0 = place(tiles.reshape(TOKENS, channels), patch_index.reshape(1, TOKENS), pos_table)
    low = lax.ppermute(x0, SEQ, [(i, i + 1) for i in range(seqs - 1)])
    high = lax.ppermute(x0, SEQ, [(i + 1, i) for i in range(seqs - 1)])
    edges = jnp.stack([(seq > 0).astype(jnp.int32), (seq < seqs - 1).astype(jnp.int32)])
    latent = encoder(edges, low, x0, high, depth_kernel, enc_gain, point_weight)

    latents = lax.all_to_all(
        jnp.broadcast_to(latent, (CLIPS, *latent.shape)), DP, split_axis=0, concat_axis=0, tiled=True
    ).reshape(CLIPS * TOKENS, channels)
    pick = (action_ids.reshape(-1)[:, None] == jnp.arange(16, dtype=jnp.int32)[None]).astype(BF)
    embeds = [embed(latents, pick, a, b) for a, b in zip(mine, others)]
    where = jnp.stack([lax.axis_index("x"), lax.axis_index("c")]).astype(jnp.int32)
    out = mix(where, seq_order, [e[0] for e in embeds], weight, [e[1] for e in embeds])
    return out.reshape(CLIPS, FRAMES, 2, COLS, -1)


def solution(mesh):
    fine = Mesh(mesh.devices.reshape(2, 4, 4, 4, 2), ("zl", "x", "zh", "y", "c"))
    placed = (
        P(DP, None, SEQ, None, None), P(DP, None, SEQ, None), P(), P(), P(), P(), P(),
        P(SEQ, DP), P(None, DP), P(DP), P(SEQ, DP), P(SEQ, None, DP), P(),
    )
    return jax.shard_map(
        body, mesh=fine, in_specs=placed, out_specs=P(None, None, SEQ, None, DP), check_vma=False
    )
```

```python
import functools

import jax
import jax.numpy as jnp
from jax import lax
from jax.experimental import pallas as pl
from jax.experimental.pallas import tpu as pltpu
from jax.sharding import Mesh
from jax.sharding import PartitionSpec as P

DIM = 5120
HEAD = 128
GROUP = 5
FRAMES = 16
COLS = 4
TOKENS = 128
CLIPS = 8
BF = jnp.bfloat16
F32 = jnp.float32
VMEM_LIMIT = 28 * 1024 * 1024
SEQ = ("zh", "y", "c")
DP = ("zl", "x")


def params(**kw):
    return pltpu.CompilerParams(vmem_limit_bytes=VMEM_LIMIT, **kw)


def cost(flops, bytes_accessed, transcendentals=0):
    return pl.CostEstimate(
        flops=int(flops), bytes_accessed=int(bytes_accessed), transcendentals=int(transcendentals)
    )


def gelu(x):
    inner = x * (0.7978845608028654 + 0.035677408136300125 * (x * x))
    half = 0.5 * x
    return half + half * jnp.tanh(inner)


def conv_norm(shifted, conv, kernel, gain, rows):
    channels = conv.shape[-1]
    total = jnp.zeros((rows * COLS, FRAMES, 128), F32)

    def step(block, total):
        lanes = pl.ds(pl.multiple_of(block * 128, 128), 128)
        taps = kernel[:, lanes].astype(F32)
        squares = []
        for r in range(rows):
            for w in range(COLS):
                acc = jnp.zeros((FRAMES, 128), F32)
                for k in range(3):
                    if not 0 <= w + k - 1 < COLS:
                        continue
                    for b in range(3):
                        for a in range(3):
                            tap = 9 * a + 3 * b + k
                            acc = acc + shifted[a, r + b, w + k - 1, :, lanes] * taps[tap : tap + 1]
                conv[r * COLS + w, :, lanes] = acc
                squares.append(acc * acc)
        return total + jnp.stack(squares)

    total = lax.fori_loop(0, channels // 128, step, total)
    mean = jnp.sum(total, axis=-1, keepdims=True) / channels
    factor = lax.rsqrt(mean + 1e-05)
    return (conv[: rows * COLS] * factor * gain.astype(F32)).astype(BF)


def shift_into(shifted, row, value):
    frame = lax.broadcasted_iota(jnp.int32, value.shape, 1)
    shifted[2, row] = value
    shifted[1, row] = jnp.where(frame >= 1, pltpu.roll(value, 1, 1), 0.0)
    shifted[0, row] = jnp.where(frame >= 2, pltpu.roll(value, 2, 1), 0.0)


def encoder_kernel(edge_ref, low_ref, own_ref, high_ref, depth_ref, gain_ref, weight_ref, out_ref, shifted, conv):
    row_tokens = COLS * FRAMES
    channels = own_ref.shape[-1]
    row = lax.broadcasted_iota(jnp.int32, (TOKENS, TOKENS), 0)
    col = lax.broadcasted_iota(jnp.int32, (TOKENS, TOKENS), 1)
    order = (col == (row & 15) * 8 + (row >> 4)).astype(BF)
    for i, ref in enumerate((low_ref, own_ref, high_ref)):
        x = jnp.dot(order, ref[...], preferred_element_type=F32)
        for half in range(2):
            part = x[half * row_tokens : (half + 1) * row_tokens]
            shift_into(shifted, 2 * i + half, part.reshape(COLS, FRAMES, channels))
    normed = conv_norm(shifted, conv, depth_ref.at[0], gain_ref[0:1], 4)
    projected = jnp.dot(normed.reshape(4 * row_tokens, channels), weight_ref[0], preferred_element_type=F32)
    hidden = []
    for i in range(4):
        x = shifted[2, i + 1].reshape(row_tokens, channels)
        x = x + gelu(projected[i * row_tokens : (i + 1) * row_tokens])
        x = x.astype(BF).astype(F32)
        if i == 0:
            x = jnp.where(edge_ref[0] == 0, 0.0, x)
        if i == 3:
            x = jnp.where(edge_ref[1] == 0, 0.0, x)
        hidden.append(x)
    for row, x in enumerate(hidden):
        shift_into(shifted, row, x.reshape(COLS, FRAMES, channels))
    normed = conv_norm(shifted, conv, depth_ref.at[1], gain_ref[1:2], 2)
    projected = jnp.dot(normed.reshape(2 * row_tokens, channels), weight_ref[1], preferred_element_type=F32)
    centre = shifted[2, 1:3].reshape(2 * row_tokens, channels)
    latent = (centre + gelu(projected)).astype(BF)
    place = lax.broadcasted_iota(jnp.int32, (channels, channels), 1)
    source = ((edge_ref[2] + ((place >> 6) & 3)) & 3) * 4 + ((edge_ref[3] + (place >> 8)) & 3)
    source = source * 64 + (place & 63)
    order = (lax.broadcasted_iota(jnp.int32, (channels, channels), 0) == source).astype(BF)
    out_ref[...] = jnp.dot(latent, order, preferred_element_type=F32).astype(BF)


def encoder(edges, low, own, high, depth_kernel, gains, weights):
    channels = own.shape[-1]
    vmem = pl.BlockSpec(memory_space=pltpu.VMEM)
    return pl.pallas_call(
        encoder_kernel,
        out_shape=jax.ShapeDtypeStruct(own.shape, BF),
        in_specs=[pl.BlockSpec(memory_space=pltpu.SMEM)] + [vmem] * 6,
        out_specs=vmem,
        scratch_shapes=[
            pltpu.VMEM((3, 6, COLS, FRAMES, channels), F32),
            pltpu.VMEM((4 * COLS, FRAMES, channels), F32),
        ],
        compiler_params=params(),
        cost_estimate=cost(2 * 384 * 1024 * 1024 * 4, 6 * 2**20),
        name="encoder",
    )(edges, low, own, high, depth_kernel, gains, weights)


def stage_kernel(parts, counts, where_ref, clip_ref, order_ref, pick_ref, latent_ref, *refs):
    pieces, (weight_ref, *refs) = refs[: 2 * sum(counts)], refs[2 * sum(counts) :]
    last = 2 in parts
    if last:
        acc_ref, total_ref, out_ref, result, out_sem, *refs = refs
        acc, squares_ref, *refs = refs
    else:
        acc, squares_ref, *refs = refs
    latent, w_in, value_ref, weight, sem, piece_sem, weight_sem = refs
    tokens, channels = latent.shape
    width = w_in.shape[3]
    cells = tokens // TOKENS
    tile = 256
    rows = weight_ref.shape[1] // 4

    loads = [pltpu.make_async_copy(latent_ref, latent, sem.at[0])]
    piece_loads, weight_loads = [], []
    taken = 0
    for i, part in enumerate(parts):
        mine = []
        for side in range(2):
            top = 0
            for k in range(counts[i]):
                ref = pieces[taken]
                taken += 1
                target = w_in.at[i, side, pl.ds(top, ref.shape[0])]
                mine.append(pltpu.make_async_copy(ref, target, piece_sem.at[i, side, k]))
                top += ref.shape[0]
        piece_loads.append(mine)
        mine = []
        for k in range(8):
            side = where_ref[1] if k < 4 else 1 - where_ref[1]
            block = side * 4 + (where_ref[0] + part) % 4
            place = ((block % 2) * 2 + k // 2 % 2) * 2 + k % 2
            source = weight_ref.at[place, pl.ds(pl.multiple_of(block // 2 * rows, rows), rows)]
            target = weight.at[i, pl.ds(k * rows, rows)]
            mine.append(pltpu.make_async_copy(source, target, weight_sem.at[i, k]))
        weight_loads.append(mine)
    if last:
        loads.append(pltpu.make_async_copy(acc_ref, acc, sem.at[1]))
    for copy in loads[:1] + [c for i in range(len(parts)) for c in piece_loads[i] + weight_loads[i]] + loads[1:]:
        copy.start()
    loads[0].wait()

    def columns_of(i, start, low, high):
        sides = []
        for side in range(2):
            left, right = max(start - side * width, 0), min(start + tile - side * width, width)
            if left < right:
                sides.append(w_in[i, side, low:high, left:right])
        return sides[0] if len(sides) == 1 else jnp.concatenate(sides, axis=1)

    total = total_ref[...] if last else jnp.zeros((tokens, 128), F32)
    for i in range(len(parts)):
        for copy in piece_loads[i]:
            copy.wait()
        for start in range(0, 2 * width, tile):
            side = columns_of(i, start, channels, channels + 16)
            action = jnp.dot(pick_ref[...], side, preferred_element_type=F32)
            gain = side[8:9].astype(F32)
            product = jnp.dot(latent[...], columns_of(i, start, 0, channels), preferred_element_type=F32)
            product = product.reshape(cells, TOKENS // FRAMES, FRAMES, tile)
            value = gelu((product + action.reshape(cells, 1, FRAMES, tile)).reshape(tokens, tile))
            squares = value * value
            total = total + (squares[:, :128] + squares[:, 128:])
            value_ref[i % 2, :, start : start + tile] = (value * gain).astype(BF)
        for copy in weight_loads[i]:
            copy.wait()
        if i == 0 and last:
            loads[1].wait()
        whole = weight.shape[2]
        for start in range(0, whole, tile):
            columns = slice(start, min(whole, start + tile))
            product = jnp.dot(value_ref[i % 2], weight[i, :, columns], preferred_element_type=F32)
            acc[:, columns] = acc[:, columns] + product if i or last else product
    squares_ref[...] = total
    if last:
        mix(clip_ref, order_ref, acc, squares_ref, out_ref, result, out_sem)


def mix(clip_ref, order_ref, acc, squares_ref, out_ref, result, out_sem):
    row = lax.broadcasted_iota(jnp.int32, (TOKENS, TOKENS), 0)
    col = lax.broadcasted_iota(jnp.int32, (TOKENS, TOKENS), 1)
    causal = ((row >> 4) == (col >> 4)) & ((col & 15) <= (row & 15))
    row = lax.broadcasted_iota(jnp.int32, (2 * TOKENS, TOKENS), 0)
    col = lax.broadcasted_iota(jnp.int32, (2 * TOKENS, TOKENS), 1)
    slot = row & 3
    source = jnp.where(
        slot < 2,
        jnp.where(slot == 0, order_ref[0], order_ref[1]),
        jnp.where(slot == 2, order_ref[2], order_ref[3]),
    )
    order = (col == (((row >> 3) & 1) * 4 + source) * 16 + (row >> 4)).astype(BF)
    ones = jnp.ones((HEAD, HEAD), BF)

    def unit(x):
        mean = jnp.dot((x * x).astype(BF), ones, preferred_element_type=F32) * (1.0 / HEAD)
        return x * lax.rsqrt(mean + 1e-06)

    def clip(c, _):
        rows = pl.ds(pl.multiple_of(c * TOKENS, TOKENS), TOKENS)
        total = jnp.sum(squares_ref[rows], axis=-1, keepdims=True)
        factor = lax.rsqrt(total / DIM + 1e-05)
        heads = [acc[rows, h * HEAD : (h + 1) * HEAD] * factor for h in range(GROUP + 2)]
        units = unit(jnp.concatenate(heads[: GROUP + 1], axis=0))
        queries = units[: GROUP * TOKENS].astype(BF)
        key = (units[GROUP * TOKENS :] * HEAD ** (-0.5)).astype(BF)
        value = jnp.concatenate([heads[GROUP + 1].astype(BF), ones], axis=1)
        score = lax.dot_general(queries, key, (((1,), (1,)), ((), ())), preferred_element_type=F32)
        raised = jnp.where(causal, jnp.exp(score).reshape(GROUP, TOKENS, TOKENS), 0.0)
        raised = raised.reshape(GROUP * TOKENS, TOKENS).astype(BF)
        both = jnp.dot(raised, value, preferred_element_type=F32)
        mixed = (both[:, :HEAD] / both[:, HEAD:]).astype(BF)
        mixed = jnp.concatenate(
            [mixed[h * TOKENS : (h + 1) * TOKENS] for h in range(GROUP)], axis=1
        )
        placed = jnp.dot(order, mixed, preferred_element_type=F32)
        placed = placed.reshape(FRAMES, 2, 2 * COLS, GROUP * HEAD)[:, :, :COLS]
        result[c] = placed.astype(BF)
        pltpu.make_async_copy(result.at[c], out_ref.at[clip_ref[c]], out_sem.at[c]).start()
        return 0

    lax.fori_loop(0, CLIPS, clip, 0, unroll=2)

    def finish(c, _):
        pltpu.make_async_copy(result.at[c], out_ref.at[clip_ref[c]], out_sem.at[c]).wait()
        return 0

    lax.fori_loop(0, CLIPS, finish, 0)


def stage(where, clips, order, pick, latent, weight, parts, pieces, carry=()):
    tokens, channels = latent.shape
    rows, width = channels + 16, pieces[0][0][0].shape[1]
    whole = weight.shape[2]
    smem, vmem = pl.BlockSpec(memory_space=pltpu.SMEM), pl.BlockSpec(memory_space=pltpu.VMEM)
    anywhere = pl.BlockSpec(memory_space=pltpu.HBM)
    sums = jax.ShapeDtypeStruct((tokens, whole), F32), jax.ShapeDtypeStruct((tokens, 128), F32)
    out = jax.ShapeDtypeStruct((CLIPS, FRAMES, 2, COLS, GROUP * HEAD), BF)
    scratch = [
        pltpu.VMEM(latent.shape, BF),
        pltpu.VMEM((len(parts), 2, rows, width), BF),
        pltpu.VMEM((2, tokens, 2 * width), BF),
        pltpu.VMEM((len(parts), 2 * width, whole), BF),
        pltpu.SemaphoreType.DMA((2,)),
        pltpu.SemaphoreType.DMA((len(parts), 2, 2)),
        pltpu.SemaphoreType.DMA((len(parts), 8)),
    ]
    if carry:
        mixing = [pltpu.VMEM(out.shape, BF), pltpu.SemaphoreType.DMA((CLIPS,))]
        scratch = mixing + [pltpu.VMEM(a.shape, F32) for a in sums] + scratch
    flat = [a for pair in pieces for piece in pair for a in piece]
    counts = tuple(len(pair[0]) for pair in pieces)
    return pl.pallas_call(
        functools.partial(stage_kernel, parts, counts),
        out_shape=out if carry else sums,
        in_specs=[smem] * 3 + [vmem] + [anywhere] * (2 + len(flat)) + [anywhere, vmem][: len(carry)],
        out_specs=anywhere if carry else (vmem, vmem),
        scratch_shapes=scratch,
        compiler_params=pltpu.CompilerParams(vmem_limit_bytes=STAGE_VMEM),
        cost_estimate=cost(len(parts) * 2 * tokens * 2 * width * (channels + whole), 12 * 2**20),
        name="stage",
    )(where, clips, order, pick, latent, *flat, weight, *carry)


STAGE_VMEM = 50 * 2**20


def shift(a, axis, by):
    n = lax.axis_size(axis)
    return lax.ppermute(a, axis, [(i, (i + by) % n) for i in range(n)])


def from_(a, axis, k):
    return shift(a, axis, -k)


def join_kernel(*refs):
    start = 0
    for ref in refs[:-1]:
        refs[-1][start : start + ref.shape[0]] = ref[...]
        start += ref.shape[0]


def join(*arrays):
    rows = sum(a.shape[0] for a in arrays)
    vmem = pl.BlockSpec(memory_space=pltpu.VMEM)
    return pl.pallas_call(
        join_kernel,
        out_shape=jax.ShapeDtypeStruct((rows, *arrays[0].shape[1:]), BF),
        in_specs=[vmem] * len(arrays),
        out_specs=vmem,
        compiler_params=pltpu.CompilerParams(vmem_limit_bytes=2**22),
        cost_estimate=cost(0, 2 * rows * 2 * arrays[0].shape[1]),
        name="join",
    )(*arrays)


def sides(a, axis):
    return from_(a, axis, 1), from_(a, axis, -1)


def across(plus, minus, axis, cut):
    return from_(minus[:cut], axis, -1), from_(plus[cut:], axis, 1)


def w_in_rows(w, side):
    zl = lax.axis_index("zl")
    mine = jnp.concatenate([w, side], 0)
    same = lax.ppermute(mine, ("zl", "c"), [(2 * z + k, 2 * k + z) for z in range(2) for k in range(2)])
    rest = lax.ppermute(w, ("zl", "c"), [(2 * z + k, 2 * (1 - k) + z) for z in range(2) for k in range(2)])
    rows = w.shape[0]
    same, side = same[:rows], same[rows:]
    block = jnp.where(zl == 0, jnp.concatenate([same, rest], 0), jnp.concatenate([rest, same], 0))
    return block, side, [from_(block, "zh", k) for k in (1, 2, 3)]


def body(
    tiles, patch_index, pos_table, depth_kernel, enc_gain, point_weight, action_ids,
    w_in, action_table, dyn_gain, w_query, w_keyval, seq_order,
):
    channels = tiles.shape[-1]
    seq = lax.axis_index(SEQ)
    seqs = lax.axis_size(SEQ)
    weight = jnp.concatenate([w_query, w_keyval.reshape(w_keyval.shape[0], -1)], axis=1)
    weight = lax.all_gather(weight, "zh", axis=0, tiled=True)

    side = jnp.concatenate(
        [action_table, dyn_gain[None], jnp.zeros((7, dyn_gain.shape[0]), BF)], axis=0
    )
    block, side, zs = w_in_rows(w_in, side)

    pick = (patch_index.reshape(-1)[:, None] == jnp.arange(pos_table.shape[0], dtype=jnp.int32)).astype(BF)
    placed = jnp.dot(pick, pos_table, preferred_element_type=F32)
    x0 = (tiles.reshape(TOKENS, channels).astype(F32) + placed).astype(BF)
    low = lax.ppermute(x0, SEQ, [(i, i + 1) for i in range(seqs - 1)])
    high = lax.ppermute(x0, SEQ, [(i + 1, i) for i in range(seqs - 1)])
    edges = [seq > 0, seq < seqs - 1, lax.axis_index("zh"), lax.axis_index("y")]
    edges = jnp.stack([a.astype(jnp.int32) for a in edges])
    latent = encoder(edges, low, x0, high, depth_kernel, enc_gain, point_weight)

    *zs, latent = lax.optimization_barrier((*zs, latent))
    column = join(block, *zs)
    swapped, near_y = shift(latent, "zl", 1), sides(column, "y")
    swapped, near_y, weight = lax.optimization_barrier((swapped, near_y, weight))
    weight = lax.all_gather(weight, ("y", "c"), axis=0)
    pair = join(latent, swapped)
    near_l, far_y = sides(pair, "x"), across(*near_y, "y", 128)
    full = join(column, near_y[0], *far_y, near_y[1], side)
    near_l, full = lax.optimization_barrier((near_l, full))
    near_w = sides(full, "x")
    far_l = across(*near_l, "x", TOKENS)
    latents = join(pair, near_l[0], *far_l, near_l[1])
    other = shift(full, "c", 1)
    near_w, latents, other = lax.optimization_barrier((near_w, latents, other))

    x, c, zl, zh, y = (lax.axis_index(a) for a in ("x", "c", "zl", "zh", "y"))
    where = jnp.stack([x, c, zl, zh, y]).astype(jnp.int32)
    place = jnp.arange(CLIPS, dtype=jnp.int32)
    clips = ((zl + place) % 2) * 4 + (x + place // 2) % 4
    mine = (clips[:, None] == place[None]).astype(jnp.int32)
    ids = jnp.sum(mine[:, :, None] * action_ids[None], axis=1)
    pick = (ids.reshape(-1)[:, None] == jnp.arange(16, dtype=jnp.int32)[None]).astype(BF)
    far_w = across(*near_w, "x", 512)
    near_o = [shift(a, "c", 1) for a in near_w]
    step = functools.partial(stage, where, clips, seq_order, pick, latents, weight)
    pieces = [([full], [other])] + [([a], [b]) for a, b in zip(near_w, near_o)]
    sums = step((0, 1, 3), pieces)
    *far_w, sums = lax.optimization_barrier((*far_w, sums))
    far_o = [shift(a, "c", 1) for a in far_w]
    return step((2,), [(far_w, far_o)], sums)


def solution(mesh):
    fine = Mesh(mesh.devices.reshape(2, 4, 4, 4, 2), ("zl", "x", "zh", "y", "c"))
    placed = (
        P(DP, None, SEQ, None, None), P(DP, None, SEQ, None), P(), P(), P(), P(), P(),
        P(SEQ, DP), P(None, DP), P(DP), P(SEQ, DP), P(SEQ, None, DP), P(),
    )
    return jax.shard_map(
        body, mesh=fine, in_specs=placed, out_specs=P(None, None, SEQ, None, DP), check_vma=False
    )
```

```python
import functools

import jax
import jax.numpy as jnp
from jax import lax
from jax.experimental import pallas as pl
from jax.experimental.pallas import tpu as pltpu
from jax.sharding import Mesh
from jax.sharding import PartitionSpec as P

DIM = 5120
HEAD = 128
GROUP = 5
FRAMES = 16
COLS = 4
TOKENS = 128
CLIPS = 8
BF = jnp.bfloat16
F32 = jnp.float32
VMEM_LIMIT = 28 * 1024 * 1024
SEQ = ("zh", "y", "c")
DP = ("zl", "x")


def params(**kw):
    return pltpu.CompilerParams(vmem_limit_bytes=VMEM_LIMIT, **kw)


def cost(flops, bytes_accessed, transcendentals=0):
    return pl.CostEstimate(
        flops=int(flops), bytes_accessed=int(bytes_accessed), transcendentals=int(transcendentals)
    )


def gelu(x):
    inner = x * (0.7978845608028654 + 0.035677408136300125 * (x * x))
    half = 0.5 * x
    return half + half * jnp.tanh(inner)


def conv_norm(shifted, conv, kernel, gain, rows):
    channels = conv.shape[-1]
    total = jnp.zeros((rows * COLS, FRAMES, 128), F32)

    def step(block, total):
        lanes = pl.ds(pl.multiple_of(block * 128, 128), 128)
        taps = kernel[:, lanes].astype(F32)
        squares = []
        for r in range(rows):
            for w in range(COLS):
                acc = jnp.zeros((FRAMES, 128), F32)
                for k in range(3):
                    if not 0 <= w + k - 1 < COLS:
                        continue
                    for b in range(3):
                        for a in range(3):
                            tap = 9 * a + 3 * b + k
                            acc = acc + shifted[a, r + b, w + k - 1, :, lanes] * taps[tap : tap + 1]
                conv[r * COLS + w, :, lanes] = acc
                squares.append(acc * acc)
        return total + jnp.stack(squares)

    total = lax.fori_loop(0, channels // 128, step, total)
    mean = jnp.sum(total, axis=-1, keepdims=True) / channels
    factor = lax.rsqrt(mean + 1e-05)
    return (conv[: rows * COLS] * factor * gain.astype(F32)).astype(BF)


def shift_into(shifted, row, value):
    frame = lax.broadcasted_iota(jnp.int32, value.shape, 1)
    shifted[2, row] = value
    shifted[1, row] = jnp.where(frame >= 1, pltpu.roll(value, 1, 1), 0.0)
    shifted[0, row] = jnp.where(frame >= 2, pltpu.roll(value, 2, 1), 0.0)


def encoder_kernel(edge_ref, low_ref, own_ref, high_ref, depth_ref, gain_ref, weight_ref, out_ref, shifted, conv):
    row_tokens = COLS * FRAMES
    channels = own_ref.shape[-1]
    row = lax.broadcasted_iota(jnp.int32, (TOKENS, TOKENS), 0)
    col = lax.broadcasted_iota(jnp.int32, (TOKENS, TOKENS), 1)
    order = (col == (row & 15) * 8 + (row >> 4)).astype(BF)
    for i, ref in enumerate((low_ref, own_ref, high_ref)):
        x = jnp.dot(order, ref[...], preferred_element_type=F32)
        for half in range(2):
            part = x[half * row_tokens : (half + 1) * row_tokens]
            shift_into(shifted, 2 * i + half, part.reshape(COLS, FRAMES, channels))
    normed = conv_norm(shifted, conv, depth_ref.at[0], gain_ref[0:1], 4)
    projected = jnp.dot(normed.reshape(4 * row_tokens, channels), weight_ref[0], preferred_element_type=F32)
    hidden = []
    for i in range(4):
        x = shifted[2, i + 1].reshape(row_tokens, channels)
        x = x + gelu(projected[i * row_tokens : (i + 1) * row_tokens])
        x = x.astype(BF).astype(F32)
        if i == 0:
            x = jnp.where(edge_ref[0] == 0, 0.0, x)
        if i == 3:
            x = jnp.where(edge_ref[1] == 0, 0.0, x)
        hidden.append(x)
    for row, x in enumerate(hidden):
        shift_into(shifted, row, x.reshape(COLS, FRAMES, channels))
    normed = conv_norm(shifted, conv, depth_ref.at[1], gain_ref[1:2], 2)
    projected = jnp.dot(normed.reshape(2 * row_tokens, channels), weight_ref[1], preferred_element_type=F32)
    centre = shifted[2, 1:3].reshape(2 * row_tokens, channels)
    latent = (centre + gelu(projected)).astype(BF)
    place = lax.broadcasted_iota(jnp.int32, (channels, channels), 1)
    source = ((edge_ref[2] + ((place >> 6) & 3)) & 3) * 4 + ((edge_ref[3] + (place >> 8)) & 3)
    source = source * 64 + (place & 63)
    order = (lax.broadcasted_iota(jnp.int32, (channels, channels), 0) == source).astype(BF)
    out_ref[...] = jnp.dot(latent, order, preferred_element_type=F32).astype(BF)


def encoder(edges, low, own, high, depth_kernel, gains, weights):
    channels = own.shape[-1]
    vmem = pl.BlockSpec(memory_space=pltpu.VMEM)
    return pl.pallas_call(
        encoder_kernel,
        out_shape=jax.ShapeDtypeStruct(own.shape, BF),
        in_specs=[pl.BlockSpec(memory_space=pltpu.SMEM)] + [vmem] * 6,
        out_specs=vmem,
        scratch_shapes=[
            pltpu.VMEM((3, 6, COLS, FRAMES, channels), F32),
            pltpu.VMEM((4 * COLS, FRAMES, channels), F32),
        ],
        compiler_params=params(),
        cost_estimate=cost(2 * 384 * 1024 * 1024 * 4, 6 * 2**20),
        name="encoder",
    )(edges, low, own, high, depth_kernel, gains, weights)


def stage_kernel(parts, counts, where_ref, clip_ref, order_ref, pick_ref, latent_ref, *refs):
    pieces, (weight_ref, *refs) = refs[: 2 * sum(counts)], refs[2 * sum(counts) :]
    last = 2 in parts
    if last:
        acc_ref, total_ref, out_ref, result, out_sem, *refs = refs
        acc, squares_ref, *refs = refs
    else:
        acc, squares_ref, *refs = refs
    latent, w_in, value_ref, weight, sem, piece_sem, weight_sem = refs
    tokens, channels = latent.shape
    width = w_in.shape[3]
    cells = tokens // TOKENS
    tile = 256
    rows = weight_ref.shape[1] // 4

    loads = [pltpu.make_async_copy(latent_ref, latent, sem.at[0])]
    piece_loads, weight_loads = [], []
    taken = 0
    for i, part in enumerate(parts):
        mine = []
        for side in range(2):
            top = 0
            for k in range(counts[i]):
                ref = pieces[taken]
                taken += 1
                target = w_in.at[i, side, pl.ds(top, ref.shape[0])]
                mine.append(pltpu.make_async_copy(ref, target, piece_sem.at[i, side, k]))
                top += ref.shape[0]
        piece_loads.append(mine)
        mine = []
        for k in range(8):
            side = where_ref[1] if k < 4 else 1 - where_ref[1]
            block = side * 4 + (where_ref[0] + part) % 4
            place = ((block % 2) * 2 + k // 2 % 2) * 2 + k % 2
            source = weight_ref.at[place, pl.ds(pl.multiple_of(block // 2 * rows, rows), rows)]
            target = weight.at[i, pl.ds(k * rows, rows)]
            mine.append(pltpu.make_async_copy(source, target, weight_sem.at[i, k]))
        weight_loads.append(mine)
    if last:
        loads.append(pltpu.make_async_copy(acc_ref, acc, sem.at[1]))
    for copy in loads[:1] + [c for i in range(len(parts)) for c in piece_loads[i] + weight_loads[i]] + loads[1:]:
        copy.start()
    loads[0].wait()

    def columns_of(i, start, low, high):
        sides = []
        for side in range(2):
            left, right = max(start - side * width, 0), min(start + tile - side * width, width)
            if left < right:
                sides.append(w_in[i, side, low:high, left:right])
        return sides[0] if len(sides) == 1 else jnp.concatenate(sides, axis=1)

    total = total_ref[...] if last else jnp.zeros((tokens, 128), F32)
    for i in range(len(parts)):
        for copy in piece_loads[i]:
            copy.wait()
        for start in range(0, 2 * width, tile):
            side = columns_of(i, start, channels, channels + 16)
            action = jnp.dot(pick_ref[...], side, preferred_element_type=F32)
            gain = side[8:9].astype(F32)
            product = jnp.dot(latent[...], columns_of(i, start, 0, channels), preferred_element_type=F32)
            product = product.reshape(cells, TOKENS // FRAMES, FRAMES, tile)
            value = gelu((product + action.reshape(cells, 1, FRAMES, tile)).reshape(tokens, tile))
            squares = value * value
            total = total + (squares[:, :128] + squares[:, 128:])
            value_ref[i % 2, :, start : start + tile] = (value * gain).astype(BF)
        for copy in weight_loads[i]:
            copy.wait()
        if i == 0 and last:
            loads[1].wait()
        whole = weight.shape[2]
        for start in range(0, whole, tile):
            columns = slice(start, min(whole, start + tile))
            product = jnp.dot(value_ref[i % 2], weight[i, :, columns], preferred_element_type=F32)
            acc[:, columns] = acc[:, columns] + product if i or last else product
    squares_ref[...] = total
    if last:
        mix(clip_ref, order_ref, acc, squares_ref, out_ref, result, out_sem)


def mix(clip_ref, order_ref, acc, squares_ref, out_ref, result, out_sem):
    row = lax.broadcasted_iota(jnp.int32, (TOKENS, TOKENS), 0)
    col = lax.broadcasted_iota(jnp.int32, (TOKENS, TOKENS), 1)
    causal = ((row >> 4) == (col >> 4)) & ((col & 15) <= (row & 15))
    row = lax.broadcasted_iota(jnp.int32, (2 * TOKENS, TOKENS), 0)
    col = lax.broadcasted_iota(jnp.int32, (2 * TOKENS, TOKENS), 1)
    slot = row & 3
    source = jnp.where(
        slot < 2,
        jnp.where(slot == 0, order_ref[0], order_ref[1]),
        jnp.where(slot == 2, order_ref[2], order_ref[3]),
    )
    order = (col == (((row >> 3) & 1) * 4 + source) * 16 + (row >> 4)).astype(BF)
    ones = jnp.ones((HEAD, HEAD), BF)

    def unit(x):
        mean = jnp.dot((x * x).astype(BF), ones, preferred_element_type=F32) * (1.0 / HEAD)
        return x * lax.rsqrt(mean + 1e-06)

    def clip(c, _):
        rows = pl.ds(pl.multiple_of(c * TOKENS, TOKENS), TOKENS)
        total = jnp.sum(squares_ref[rows], axis=-1, keepdims=True)
        factor = lax.rsqrt(total / DIM + 1e-05)
        heads = [acc[rows, h * HEAD : (h + 1) * HEAD] * factor for h in range(GROUP + 2)]
        units = unit(jnp.concatenate(heads[: GROUP + 1], axis=0))
        queries = units[: GROUP * TOKENS].astype(BF)
        key = (units[GROUP * TOKENS :] * HEAD ** (-0.5)).astype(BF)
        value = jnp.concatenate([heads[GROUP + 1].astype(BF), ones], axis=1)
        score = lax.dot_general(queries, key, (((1,), (1,)), ((), ())), preferred_element_type=F32)
        raised = jnp.where(causal, jnp.exp(score).reshape(GROUP, TOKENS, TOKENS), 0.0)
        raised = raised.reshape(GROUP * TOKENS, TOKENS).astype(BF)
        both = jnp.dot(raised, value, preferred_element_type=F32)
        mixed = (both[:, :HEAD] / both[:, HEAD:]).astype(BF)
        mixed = jnp.concatenate(
            [mixed[h * TOKENS : (h + 1) * TOKENS] for h in range(GROUP)], axis=1
        )
        placed = jnp.dot(order, mixed, preferred_element_type=F32)
        placed = placed.reshape(FRAMES, 2, 2 * COLS, GROUP * HEAD)[:, :, :COLS]
        result[c] = placed.astype(BF)
        pltpu.make_async_copy(result.at[c], out_ref.at[clip_ref[c]], out_sem.at[c]).start()
        return 0

    lax.fori_loop(0, CLIPS, clip, 0, unroll=2)

    def finish(c, _):
        pltpu.make_async_copy(result.at[c], out_ref.at[clip_ref[c]], out_sem.at[c]).wait()
        return 0

    lax.fori_loop(0, CLIPS, finish, 0)


def stage(where, clips, order, pick, latent, weight, parts, pieces, carry=()):
    tokens, channels = latent.shape
    rows, width = channels + 16, pieces[0][0][0].shape[1]
    whole = weight.shape[2]
    smem, vmem = pl.BlockSpec(memory_space=pltpu.SMEM), pl.BlockSpec(memory_space=pltpu.VMEM)
    anywhere = pl.BlockSpec(memory_space=pltpu.HBM)
    sums = jax.ShapeDtypeStruct((tokens, whole), F32), jax.ShapeDtypeStruct((tokens, 128), F32)
    out = jax.ShapeDtypeStruct((CLIPS, FRAMES, 2, COLS, GROUP * HEAD), BF)
    scratch = [
        pltpu.VMEM(latent.shape, BF),
        pltpu.VMEM((len(parts), 2, rows, width), BF),
        pltpu.VMEM((2, tokens, 2 * width), BF),
        pltpu.VMEM((len(parts), 2 * width, whole), BF),
        pltpu.SemaphoreType.DMA((2,)),
        pltpu.SemaphoreType.DMA((len(parts), 2, 2)),
        pltpu.SemaphoreType.DMA((len(parts), 8)),
    ]
    if carry:
        mixing = [pltpu.VMEM(out.shape, BF), pltpu.SemaphoreType.DMA((CLIPS,))]
        scratch = mixing + [pltpu.VMEM(a.shape, F32) for a in sums] + scratch
    flat = [a for pair in pieces for piece in pair for a in piece]
    counts = tuple(len(pair[0]) for pair in pieces)
    return pl.pallas_call(
        functools.partial(stage_kernel, parts, counts),
        out_shape=out if carry else sums,
        in_specs=[smem] * 3 + [vmem] + [anywhere] * (2 + len(flat)) + [anywhere, vmem][: len(carry)],
        out_specs=anywhere if carry else (vmem, vmem),
        scratch_shapes=scratch,
        compiler_params=pltpu.CompilerParams(vmem_limit_bytes=STAGE_VMEM),
        cost_estimate=cost(len(parts) * 2 * tokens * 2 * width * (channels + whole), 12 * 2**20),
        name="stage",
    )(where, clips, order, pick, latent, *flat, weight, *carry)


STAGE_VMEM = 50 * 2**20


def shift(a, axis, by):
    n = lax.axis_size(axis)
    return lax.ppermute(a, axis, [(i, (i + by) % n) for i in range(n)])


def from_(a, axis, k):
    return shift(a, axis, -k)


def join_kernel(*refs):
    start = 0
    for ref in refs[:-1]:
        refs[-1][start : start + ref.shape[0]] = ref[...]
        start += ref.shape[0]


def join(*arrays):
    rows = sum(a.shape[0] for a in arrays)
    vmem = pl.BlockSpec(memory_space=pltpu.VMEM)
    return pl.pallas_call(
        join_kernel,
        out_shape=jax.ShapeDtypeStruct((rows, *arrays[0].shape[1:]), BF),
        in_specs=[vmem] * len(arrays),
        out_specs=vmem,
        compiler_params=pltpu.CompilerParams(vmem_limit_bytes=2**22),
        cost_estimate=cost(0, 2 * rows * 2 * arrays[0].shape[1]),
        name="join",
    )(*arrays)


def cut_kernel(first_ref, second_ref, upper_ref, lower_ref):
    upper_ref[...] = first_ref[: upper_ref.shape[0]]
    lower_ref[...] = second_ref[upper_ref.shape[0] :]


def cut(first, second, row):
    vmem = pl.BlockSpec(memory_space=pltpu.VMEM)
    rows, width = first.shape
    return pl.pallas_call(
        cut_kernel,
        out_shape=[jax.ShapeDtypeStruct((n, width), BF) for n in (row, rows - row)],
        in_specs=[vmem] * 2,
        out_specs=[vmem] * 2,
        compiler_params=pltpu.CompilerParams(vmem_limit_bytes=8 * 2**20),
        cost_estimate=cost(0, 4 * rows * width),
        name="cut",
    )(first, second)


def sides(a, axis):
    return from_(a, axis, 1), from_(a, axis, -1)


def across(plus, minus, axis, cut):
    return from_(minus[:cut], axis, -1), from_(plus[cut:], axis, 1)


def w_in_rows(w, side):
    zl = lax.axis_index("zl")
    mine = jnp.concatenate([w, side], 0)
    same = lax.ppermute(mine, ("zl", "c"), [(2 * z + k, 2 * k + z) for z in range(2) for k in range(2)])
    rest = lax.ppermute(w, ("zl", "c"), [(2 * z + k, 2 * (1 - k) + z) for z in range(2) for k in range(2)])
    rows = w.shape[0]
    same, side = same[:rows], same[rows:]
    block = jnp.where(zl == 0, jnp.concatenate([same, rest], 0), jnp.concatenate([rest, same], 0))
    return block, side, [from_(block, "zh", k) for k in (1, 2, 3)]


def body(
    tiles, patch_index, pos_table, depth_kernel, enc_gain, point_weight, action_ids,
    w_in, action_table, dyn_gain, w_query, w_keyval, seq_order,
):
    channels = tiles.shape[-1]
    seq = lax.axis_index(SEQ)
    seqs = lax.axis_size(SEQ)
    weight = jnp.concatenate([w_query, w_keyval.reshape(w_keyval.shape[0], -1)], axis=1)
    weight = lax.all_gather(weight, "zh", axis=0, tiled=True)

    side = jnp.concatenate(
        [action_table, dyn_gain[None], jnp.zeros((7, dyn_gain.shape[0]), BF)], axis=0
    )
    block, side, zs = w_in_rows(w_in, side)

    pick = (patch_index.reshape(-1)[:, None] == jnp.arange(pos_table.shape[0], dtype=jnp.int32)).astype(BF)
    placed = jnp.dot(pick, pos_table, preferred_element_type=F32)
    x0 = (tiles.reshape(TOKENS, channels).astype(F32) + placed).astype(BF)
    low = lax.ppermute(x0, SEQ, [(i, i + 1) for i in range(seqs - 1)])
    high = lax.ppermute(x0, SEQ, [(i + 1, i) for i in range(seqs - 1)])
    edges = [seq > 0, seq < seqs - 1, lax.axis_index("zh"), lax.axis_index("y")]
    edges = jnp.stack([a.astype(jnp.int32) for a in edges])
    latent = encoder(edges, low, x0, high, depth_kernel, enc_gain, point_weight)

    *zs, latent = lax.optimization_barrier((*zs, latent))
    column = join(block, *zs)
    swapped, near_y = shift(latent, "zl", 1), sides(column, "y")
    swapped, near_y, weight = lax.optimization_barrier((swapped, near_y, weight))
    weight = lax.all_gather(weight, ("y", "c"), axis=0)
    pair = join(latent, swapped)
    near_l, far_y = sides(pair, "x"), across(*near_y, "y", 128)
    full = join(column, near_y[0], *far_y, near_y[1], side)
    near_l, full = lax.optimization_barrier((near_l, full))
    near_w = sides(full, "x")
    far_l = across(*near_l, "x", TOKENS)
    latents = join(pair, near_l[0], *far_l, near_l[1])
    other = shift(full, "c", 1)
    near_w, latents, other = lax.optimization_barrier((near_w, latents, other))

    x, c, zl, zh, y = (lax.axis_index(a) for a in ("x", "c", "zl", "zh", "y"))
    where = jnp.stack([x, c, zl, zh, y]).astype(jnp.int32)
    place = jnp.arange(CLIPS, dtype=jnp.int32)
    clips = ((zl + place) % 2) * 4 + (x + place // 2) % 4
    mine = (clips[:, None] == place[None]).astype(jnp.int32)
    ids = jnp.sum(mine[:, :, None] * action_ids[None], axis=1)
    pick = (ids.reshape(-1)[:, None] == jnp.arange(16, dtype=jnp.int32)[None]).astype(BF)
    upper, lower = cut(near_w[1], near_w[0], 512)
    far_w = [from_(upper, "x", -1), from_(lower, "x", 1)]
    near_o = [shift(a, "c", 1) for a in near_w]
    step = functools.partial(stage, where, clips, seq_order, pick, latents, weight)
    pieces = [([full], [other])] + [([a], [b]) for a, b in zip(near_w, near_o)]
    sums = step((0, 1, 3), pieces)
    *far_w, sums = lax.optimization_barrier((*far_w, sums))
    far_o = [shift(a, "c", 1) for a in far_w]
    return step((2,), [(far_w, far_o)], sums)


def solution(mesh):
    fine = Mesh(mesh.devices.reshape(2, 4, 4, 4, 2), ("zl", "x", "zh", "y", "c"))
    placed = (
        P(DP, None, SEQ, None, None), P(DP, None, SEQ, None), P(), P(), P(), P(), P(),
        P(SEQ, DP), P(None, DP), P(DP), P(SEQ, DP), P(SEQ, None, DP), P(),
    )
    return jax.shard_map(
        body, mesh=fine, in_specs=placed, out_specs=P(None, None, SEQ, None, DP), check_vma=False
    )
```
